256 devices in a mesh: ctx: 16 (over z, x_lo), head: 16 (over x_hi, y, core).
Axes of the slice: x: 4 (x_hi: 2, x_lo: 2; x = x_hi * 2 + x_lo), y: 4, z: 8, core: 2. Of those that a mesh axis runs over, the one named last changes fastest.
Arguments:
- queries: bfloat16 [32768, 64, 128], P(('ctx', 'head')), may hold values from -100 to 100
- keys: bfloat16 [32768, 8, 128], P(('ctx', 'head')), may hold values from -6 to 6
- values: bfloat16 [32768, 8, 128], P(('ctx', 'head')), may hold values from -6 to 6
- outputs: bfloat16 [32768, 64, 128], P(('ctx', 'head')), may hold values from -6 to 6
- out_grad: bfloat16 [32768, 64, 128], P(('ctx', 'head')), may hold values from -6 to 6
- segments: int32 [32768], replicated, may hold values from 0 to 255, never falling along the last dimension, each value on 1 to 512 neighbouring positions
Outputs:
- query_grad: bfloat16 [32768, 64, 128], P(('ctx', 'head'))
- key_grad: bfloat16 [32768, 8, 128], P(('ctx', 'head'))
- value_grad: bfloat16 [32768, 8, 128], P(('ctx', 'head'))
The draws below stay inside these ranges and needn't reach their ends.
Inputs may be any that keep to these rules, and one draw needn't show every extreme that they name: `segments`: the document number never falls along the pack; every document has 1 to 512 tokens and one has exactly 512.
All inputs are finite; a program needn't handle non-finite values.
Results may differ from the reference program's by a relative error of at most 0.007.
Values may be sent and summed in bfloat16 or wider, within the bound.
No kernel may reach another device: no remote copies, remote signals or barrier semaphores. Data moves between devices by JAX's collectives and lax.ppermute only.
A program may use at most 128 MiB of HBM per device.

```python
import math
import jax
import jax.numpy as jnp
import numpy as np
from jax import lax

QH = 64
KVH = 8
HD = 128
TOKENS = 32768
DOC_MOST = 512
NDOCS = 256
BLOCK = 512


def draw_pair(key):
    base_key = jax.random.fold_in(key, 7001)
    first, second = jax.random.split(base_key, 2)
    key_rows = jax.random.truncated_normal(first, -4.5, 4.5, (TOKENS, KVH, HD), jnp.float32)
    query_rows = jax.random.truncated_normal(second, -4.5, 4.5, (TOKENS, QH, HD), jnp.float32)
    return (query_rows, key_rows)


def draw_queries(key, part):
    return draw_pair(key)[0].astype(jnp.bfloat16)


def draw_keys(key, part):
    return draw_pair(key)[1].astype(jnp.bfloat16)


def block_levels(stream_key, shape, cuts, low, high):
    def one(position, blocks):
        draws = jax.random.uniform(jax.random.fold_in(jax.random.fold_in(stream_key, 6), position), (blocks,), jnp.float32, low / len(cuts), high / len(cuts))
        return jnp.repeat(jnp.exp(draws), shape[position] // blocks).reshape((-1,) + (1,) * (len(shape) - position - 1))

    level = one(*cuts[0])
    for cut in cuts[1:]:
        level = level * one(*cut)
    return level


def length_profile(number_of, total, bound, slope):
    weights = [(1 << 20) // math.isqrt(rank ** slope) + 1 for rank in range(2, number_of + 1)]
    spare, counts = total - bound - (number_of - 1), [1] * (number_of - 1)
    while spare > 0:
        free = [i for i in range(number_of - 1) if counts[i] < bound]
        mass, budget = sum([weights[i] for i in free]), spare
        for i in free:
            more = min(bound - counts[i], max(1, budget * weights[i] // mass), spare)
            counts[i] = counts[i] + more
            spare = spare - more
    return np.array([bound] + counts)


def uneven_parts(own_key, amount, total, reach, skew):
    if amount == 2:
        one = jax.random.randint(own_key, (), max(1, total - reach), min(reach, total - 1) + 1)
        return jnp.stack([one, total - one])
    tallies = jnp.asarray(length_profile(amount, total, reach, skew), jnp.int32)
    twos = (amount - 1) // 2
    donor, taker = tallies[1:1 + 2 * twos:2], tallies[2:2 + 2 * twos:2]
    margin = jnp.minimum(donor - 1, reach - taker)
    passed = jax.random.randint(jax.random.fold_in(own_key, 1), (twos,), 0, 1 << 20) % (margin + 1)
    tallies = tallies.at[1:1 + 2 * twos:2].set(donor - passed).at[2:2 + 2 * twos:2].set(taker + passed)
    return tallies[jax.random.permutation(jax.random.fold_in(own_key, 2), amount)]


def normal_values(own_key, extent, scale, limit, shards=(), held_as=jnp.bfloat16):
    gain = block_levels(own_key, extent, shards, -0.22, 0.18) if shards else 1.0
    values = jax.random.normal(own_key, extent, jnp.float32) * scale * gain
    return jnp.minimum(jnp.maximum(values, -limit), limit).astype(held_as)


def setup_inputs(seed: int = 0) -> dict:
    streams_of = jax.random.split(jax.random.key(seed), 7)
    queries = draw_queries(jax.random.fold_in(streams_of[6], 71), 0)
    keys = draw_keys(jax.random.fold_in(streams_of[6], 71), 0)
    values = normal_values(streams_of[2], (TOKENS, KVH, HD), 1.0, 6.0, ((0, 256),))
    outputs = normal_values(streams_of[3], (TOKENS, QH, HD), 1.0, 6.0, ((0, 256),))
    out_grad = normal_values(streams_of[4], (TOKENS, QH, HD), 1.0, 6.0, ((0, 256),))
    segments = jnp.searchsorted(jnp.cumsum(uneven_parts(streams_of[5], NDOCS, TOKENS, DOC_MOST, 2)), jnp.arange(TOKENS), side="right").astype(jnp.int32)
    return dict(queries=queries, keys=keys, values=values, outputs=outputs, out_grad=out_grad, segments=segments)


def reference(queries, keys, values, outputs, out_grad, segments):
    group = QH // KVH
    scale = HD ** -0.5
    window = DOC_MOST + BLOCK
    delta_all = jnp.sum(out_grad.astype(jnp.float32) * outputs.astype(jnp.float32), axis=2)
    keys_pad = jnp.concatenate([jnp.zeros((DOC_MOST, KVH, HD), keys.dtype), keys], axis=0)
    values_pad = jnp.concatenate([jnp.zeros((DOC_MOST, KVH, HD), values.dtype), values], axis=0)
    seg_pad = jnp.concatenate([jnp.full((DOC_MOST,), -1, jnp.int32), segments.astype(jnp.int32)], axis=0)
    row_index = jnp.arange(BLOCK, dtype=jnp.int32)
    col_index = jnp.arange(window, dtype=jnp.int32)
    causal = col_index[None, :] <= row_index[:, None] + DOC_MOST

    def one_block(carry, block_index):
        grad_keys, grad_values = carry
        start_row = (block_index * BLOCK).astype(jnp.int32)
        q_block = lax.dynamic_slice_in_dim(queries, start_row, BLOCK, 0).reshape(BLOCK, KVH, group, HD)
        g_block = lax.dynamic_slice_in_dim(out_grad, start_row, BLOCK, 0).reshape(BLOCK, KVH, group, HD)
        d_block = lax.dynamic_slice_in_dim(delta_all, start_row, BLOCK, 0).reshape(BLOCK, KVH, group)
        d_block = jnp.transpose(d_block, (1, 2, 0))
        k_window = lax.dynamic_slice_in_dim(keys_pad, start_row, window, 0)
        v_window = lax.dynamic_slice_in_dim(values_pad, start_row, window, 0)
        seg_query = lax.dynamic_slice_in_dim(segments.astype(jnp.int32), start_row, BLOCK, 0)
        seg_keys = lax.dynamic_slice_in_dim(seg_pad, start_row, window, 0)
        allowed = (seg_query[:, None] == seg_keys[None, :]) & causal
        raw = scale * jnp.einsum("bkgd,wkd->kgbw", q_block.astype(jnp.float32), k_window.astype(jnp.float32))
        masked = jnp.where(allowed, raw, -jnp.inf)
        top = jnp.max(masked, axis=-1)
        log_sum = top + jnp.log(jnp.sum(jnp.exp(masked - top[..., None]), axis=-1))
        prob = jnp.exp(masked - log_sum[..., None])
        prob_low = prob.astype(jnp.bfloat16)
        d_prob = jnp.einsum("bkgd,wkd->kgbw", g_block.astype(jnp.float32), v_window.astype(jnp.float32))
        d_score = (prob * (d_prob - d_block[..., None])).astype(jnp.bfloat16)
        query_part = scale * jnp.einsum("kgbw,wkd->bkgd", d_score.astype(jnp.float32), k_window.astype(jnp.float32))
        key_part = scale * jnp.einsum("kgbw,bkgd->wkd", d_score.astype(jnp.float32), q_block.astype(jnp.float32))
        value_part = jnp.einsum("kgbw,bkgd->wkd", prob_low.astype(jnp.float32), g_block.astype(jnp.float32))
        old_keys = lax.dynamic_slice_in_dim(grad_keys, start_row, window, 0)
        old_values = lax.dynamic_slice_in_dim(grad_values, start_row, window, 0)
        grad_keys = lax.dynamic_update_slice_in_dim(grad_keys, old_keys + key_part, start_row, 0)
        grad_values = lax.dynamic_update_slice_in_dim(grad_values, old_values + value_part, start_row, 0)
        return (grad_keys, grad_values), query_part.reshape(BLOCK, QH, HD).astype(jnp.bfloat16)

    start_keys = jnp.zeros((TOKENS + DOC_MOST, KVH, HD), jnp.float32)
    start_values = jnp.zeros((TOKENS + DOC_MOST, KVH, HD), jnp.float32)
    (grad_keys, grad_values), query_blocks = lax.scan(one_block, (start_keys, start_values), jnp.arange(TOKENS // BLOCK, dtype=jnp.int32))
    query_grad = query_blocks.reshape(TOKENS, QH, HD)
    return query_grad, grad_keys[DOC_MOST:].astype(jnp.bfloat16), grad_values[DOC_MOST:].astype(jnp.bfloat16)
```

```python
import functools
import math

import jax
import jax.numpy as jnp
from jax import lax
from jax.experimental import pallas as pl
from jax.experimental.pallas import tpu as pltpu
from jax.sharding import PartitionSpec as P

AXES = ("ctx", "head")
BLK = 128
NEG = -1e30
CHUNKS = 4
LANES = 256


def chip_shift(x, chips):
    n = lax.axis_size("ctx") * lax.axis_size("head")
    return lax.ppermute(x, AXES, [(i, (i + 2 * chips) % n) for i in range(n)])


def swap_cores(x):
    n = lax.axis_size("ctx") * lax.axis_size("head")
    return lax.ppermute(x, AXES, [(i, i ^ 1) for i in range(n)])


def chunk_kernel(
    scal, q_own, q_twin, g_own, g_twin, d_own, d_twin, start, kv_own, kv_a, kv_b,
    dq_own, dq_twin, dkv_own, dkv_a, dkv_b,
    qs, gs, ds_, kbuf, vbuf, ktr, dk, dv,
):
    core = scal[0]
    scale = HDSCALE
    rows = qs.shape[1]
    for slot, (q, g, d) in enumerate(((q_own, g_own, d_own), (q_twin, g_twin, d_twin))):
        qs[slot] = q[...].astype(jnp.float32).reshape(rows, BLK).astype(jnp.bfloat16)
        gs[slot] = g[...].astype(jnp.float32).reshape(rows, BLK).astype(jnp.bfloat16)
        ds_[slot] = d[...]
    for n, src in enumerate((kv_b, kv_a, kv_own)):
        kbuf[256 * n : 256 * (n + 1), :] = src[0]
        vbuf[256 * n : 256 * (n + 1), :] = src[1]
        ktr[:, 256 * n : 256 * (n + 1)] = src[0].T
    dk[...] = jnp.zeros_like(dk)
    dv[...] = jnp.zeros_like(dv)

    for rb in range(2):
        slot = jnp.where(core == rb, 0, 1)
        k0 = rb * BLK
        kwin = kbuf[k0 : k0 + 5 * BLK, :]
        vwin = vbuf[k0 : k0 + 5 * BLK, :]
        kt = ktr[:, k0 : k0 + 5 * BLK]

        def tile(lt, _):
            base = pl.multiple_of(lt * LANES, LANES)
            q_t = qs[slot, pl.ds(base, LANES), :]
            g_t = gs[slot, pl.ds(base, LANES), :]
            del_t = ds_[slot, :, pl.ds(base, LANES)]
            st = start[rb, :, pl.ds(base, LANES)]
            nt = (((1,), (1,)), ((), ()))
            s = lax.dot_general(kwin, q_t, nt, preferred_element_type=jnp.float32)
            u = lax.broadcasted_iota(jnp.int32, s.shape, 0)
            tok = 4 * BLK + ((base + lax.broadcasted_iota(jnp.int32, s.shape, 1)) >> 3)
            ok = (u >= st) & (u <= tok)
            s = jnp.where(ok, s * (scale * math.log2(math.e)), NEG)
            m = jnp.max(s, axis=0, keepdims=True)
            e = jnp.exp2(s - m)
            inv = 1.0 / jnp.sum(e, axis=0, keepdims=True)
            p = e * inv
            dp = lax.dot_general(vwin, g_t, nt, preferred_element_type=jnp.float32)
            dsc = (p * (dp - del_t)).astype(jnp.bfloat16)
            dv[k0 : k0 + 5 * BLK, :] += jnp.dot(
                p.astype(jnp.bfloat16), g_t, preferred_element_type=jnp.float32
            )
            dk[k0 : k0 + 5 * BLK, :] += jnp.dot(dsc, q_t, preferred_element_type=jnp.float32)
            dqt = jnp.dot(kt, dsc, preferred_element_type=jnp.float32)
            dqv = (dqt.T * scale).reshape(LANES // 8, 8, BLK).astype(jnp.bfloat16)
            tb = pl.multiple_of(lt * (LANES // 8), LANES // 8)

            @pl.when(slot == 0)
            def _():
                dq_own[pl.ds(tb, LANES // 8)] = dqv

            @pl.when(slot == 1)
            def _():
                dq_twin[pl.ds(tb, LANES // 8)] = dqv

            return 0

        lax.fori_loop(0, rows // LANES, tile, 0)
    for n, dst in enumerate((dkv_b, dkv_a, dkv_own)):
        dst[0] = (dk[256 * n : 256 * (n + 1), :] * scale).astype(dst.dtype)
        dst[1] = dv[256 * n : 256 * (n + 1), :].astype(dst.dtype)


HDSCALE = 128 ** (-0.5)


def chunk_call(core, h0, nh, q4, qt, g4, gt, d_own, d_twin, start, kv_own, kv_a, kv_b):
    rows = BLK * 8
    own = pl.BlockSpec((BLK, None, 8, BLK), lambda h, s: (0, 4 * s[0] + h0 + h, 0, 0))
    twin = pl.BlockSpec((BLK, None, 8, BLK), lambda h, s: (0, h0 + h, 0, 0))
    d_o = pl.BlockSpec((None, 1, rows), lambda h, s: (4 * s[0] + h0 + h, 0, 0))
    d_t = pl.BlockSpec((None, 1, rows), lambda h, s: (h0 + h, 0, 0))
    st = pl.BlockSpec((2, 1, rows), lambda h, s: (0, 0, 0))
    kvo = pl.BlockSpec((None, 2, 256, BLK), lambda h, s: (h0 + h, 0, 0, 0))
    kvc = pl.BlockSpec((None, 2, 256, BLK), lambda h, s: (h, 0, 0, 0))
    dqs = pl.BlockSpec((BLK, None, 8, BLK), lambda h, s: (0, h, 0, 0))
    return pl.pallas_call(
        chunk_kernel,
        grid_spec=pltpu.PrefetchScalarGridSpec(
            num_scalar_prefetch=1,
            grid=(nh,),
            in_specs=[own, twin, own, twin, d_o, d_t, st, kvo, kvc, kvc],
            out_specs=[dqs, dqs, kvc, kvc, kvc],
            scratch_shapes=[
                pltpu.VMEM((2, rows, BLK), jnp.bfloat16),
                pltpu.VMEM((2, rows, BLK), jnp.bfloat16),
                pltpu.VMEM((2, 1, rows), jnp.float32),
                pltpu.VMEM((768, BLK), jnp.bfloat16),
                pltpu.VMEM((768, BLK), jnp.bfloat16),
                pltpu.VMEM((BLK, 768), jnp.bfloat16),
                pltpu.VMEM((768, BLK), jnp.float32),
                pltpu.VMEM((768, BLK), jnp.float32),
            ],
        ),
        out_shape=[
            jax.ShapeDtypeStruct((BLK, nh, 8, BLK), jnp.bfloat16),
            jax.ShapeDtypeStruct((BLK, nh, 8, BLK), jnp.bfloat16),
            jax.ShapeDtypeStruct((nh, 2, 256, BLK), jnp.float32),
            jax.ShapeDtypeStruct((nh, 2, 256, BLK), jnp.bfloat16),
            jax.ShapeDtypeStruct((nh, 2, 256, BLK), jnp.bfloat16),
        ],
        compiler_params=pltpu.CompilerParams(vmem_limit_bytes=40 << 20),
        cost_estimate=pl.CostEstimate(
            flops=nh * 2 * 5 * 2 * rows * 640 * 128,
            bytes_accessed=nh * (6 * rows * 256 + 7 * 131072),
            transcendentals=nh * 2 * rows * 640,
        ),
        name="attention_chunk",
    )(core.reshape(1), q4, qt, g4, gt, d_own, d_twin, start, kv_own, kv_a, kv_b)


def shards(queries, keys, values, outputs, out_grad, segments):
    head = lax.axis_index("head")
    dev = lax.axis_index("ctx") * lax.axis_size("head") + head
    core = dev % 2
    chip = dev // 2
    nh = 4 // CHUNKS

    kvt = jnp.stack(
        [jnp.transpose(keys, (1, 0, 2)), jnp.transpose(values, (1, 0, 2))], axis=1
    )
    kv2 = kvt.reshape(2, 4, 2, BLK, BLK)
    mine = lax.dynamic_index_in_dim(kv2, core, 0, keepdims=False)
    other = swap_cores(lax.dynamic_index_in_dim(kv2, 1 - core, 0, keepdims=False))
    lo = jnp.where(core == 0, mine, other)
    hi = jnp.where(core == 0, other, mine)
    kvc = jnp.concatenate([lo, hi], axis=2)

    kv_a = [chip_shift(kvc[c * nh : (c + 1) * nh], 1) for c in range(CHUNKS)]
    kv_b = [chip_shift(kvc[c * nh : (c + 1) * nh], 2) for c in range(CHUNKS)]

    q4 = queries.reshape(BLK, 8, 8, BLK)
    g4 = out_grad.reshape(BLK, 8, 8, BLK)
    qt = swap_cores(lax.dynamic_slice_in_dim(q4, 4 * (1 - core), 4, 1))
    gt = swap_cores(lax.dynamic_slice_in_dim(g4, 4 * (1 - core), 4, 1))
    delta = jnp.sum(outputs.astype(jnp.float32) * out_grad.astype(jnp.float32), axis=-1)
    delta = jnp.transpose(delta.reshape(BLK, 8, 8), (1, 0, 2)).reshape(8, 1, BLK * 8)
    d_twin = swap_cores(lax.dynamic_slice_in_dim(delta, 4 * (1 - core), 4, 0))

    seg_pad = jnp.concatenate([jnp.full((512,), -1, jnp.int32), segments])
    seg_w = lax.dynamic_slice_in_dim(seg_pad, chip * 256, 768, 0)
    first = jnp.sum((seg_w[None, :] < seg_w[512:, None]).astype(jnp.int32), axis=1)
    first = first.reshape(2, BLK) - jnp.array([[0], [BLK]], jnp.int32)
    start = jnp.broadcast_to(first[:, :, None], (2, BLK, 8)).reshape(2, 1, BLK * 8)

    dq_own, dq_twin, own, back_a, back_b = [], [], [], [], []
    for c in range(CHUNKS):
        o, t, dkv_o, dkv_a, dkv_b = chunk_call(
            core, c * nh, nh, q4, qt, g4, gt, delta, d_twin, start, kvc, kv_a[c], kv_b[c]
        )
        dq_own.append(o)
        dq_twin.append(swap_cores(t))
        own.append(dkv_o)
        back_b.append(chip_shift(dkv_b, -2))
        back_a.append(chip_shift(dkv_a, -1))
    o = jnp.concatenate(dq_own, axis=1)
    t = jnp.concatenate(dq_twin, axis=1)
    dq = jnp.concatenate(
        [jnp.where(core == 0, o, t), jnp.where(core == 0, t, o)], axis=1
    ).reshape(BLK, 64, BLK)

    total = jnp.concatenate(
        [
            (a + b.astype(jnp.float32) + c.astype(jnp.float32)).astype(jnp.bfloat16)
            for a, b, c in zip(own, back_a, back_b)
        ],
        axis=0,
    ).reshape(4, 2, 2, BLK, BLK)
    keep = lax.dynamic_index_in_dim(total, core, 2, keepdims=False)
    got = swap_cores(lax.dynamic_index_in_dim(total, 1 - core, 2, keepdims=False))
    full = jnp.concatenate(
        [jnp.where(core == 0, keep, got), jnp.where(core == 0, got, keep)], axis=0
    )
    dkeys = jnp.transpose(full[:, 0], (1, 0, 2))
    dvals = jnp.transpose(full[:, 1], (1, 0, 2))
    return dq, dkeys, dvals


def solution(mesh):
    spec = P(AXES, None, None)
    return jax.shard_map(
        shards,
        mesh=mesh,
        in_specs=(spec, spec, spec, spec, spec, P()),
        out_specs=(spec, spec, spec),
        check_vma=False,
    )
```

```python
import functools
import math

import jax
import jax.numpy as jnp
from jax import lax
from jax.experimental import pallas as pl
from jax.experimental.pallas import tpu as pltpu
from jax.sharding import PartitionSpec as P

AXES = ("ctx", "head")
BLK = 128
NEG = -1e30
SCALE = BLK ** (-0.5)
CHUNKS = (2, 2)
VMEM = 28 << 20
DELTA_VMEM = 57 << 20


def chip_shift(x, chips):
    n = lax.axis_size("ctx") * lax.axis_size("head")
    return lax.ppermute(x, AXES, [(i, (i + 2 * chips) % n) for i in range(n)])


def swap_cores(x):
    n = lax.axis_size("ctx") * lax.axis_size("head")
    return lax.ppermute(x, AXES, [(i, i ^ 1) for i in range(n)])


def gather_kernel(slot, scal, k, v, *refs):
    outs, tmp = refs[-len(CHUNKS) - 1 : -1], refs[-1]
    core = scal[0]
    rb = core if slot == 0 else 1 - core
    rows = pl.ds(pl.multiple_of(rb * BLK, BLK), BLK)
    for kind, src in enumerate((k, v)):
        tmp[...] = src[...].astype(jnp.float32).reshape(BLK * 8, BLK)
        h = 0
        for out in outs:
            for i in range(out.shape[0]):
                part = tmp[pl.ds(4 * core + h, BLK, stride=8), :]
                out[i, kind, rows, :] = part.astype(jnp.bfloat16)
                h += 1


def gather_call(core, slot, k, v, chain):
    vm = pl.BlockSpec(memory_space=pltpu.VMEM)
    return pl.pallas_call(
        functools.partial(gather_kernel, slot),
        in_specs=[pl.BlockSpec(memory_space=pltpu.SMEM)] + [vm] * (2 + len(chain)),
        out_specs=[vm] * len(CHUNKS),
        out_shape=[jax.ShapeDtypeStruct((nh, 2, 256, BLK), jnp.bfloat16) for nh in CHUNKS],
        scratch_shapes=[pltpu.VMEM((BLK * 8, BLK), jnp.float32)],
        input_output_aliases={3 + i: i for i in range(len(chain))},
        compiler_params=pltpu.CompilerParams(vmem_limit_bytes=VMEM),
        cost_estimate=pl.CostEstimate(flops=0, bytes_accessed=1 << 19, transcendentals=0),
        name="gather_heads",
    )(core, k, v, *chain)


def final_sum_kernel(scal, *refs):
    n = len(CHUNKS)
    core = scal[0]
    own, a, b = refs[:n], refs[n : 2 * n], refs[2 * n : 3 * n]
    keep, send = refs[3 * n :]
    h = 0
    for c in range(n):
        for i in range(CHUNKS[c]):
            for kind in range(2):
                for out, rb in ((keep, core), (send, 1 - core)):
                    rows = pl.ds(pl.multiple_of(rb * BLK, BLK), BLK)
                    out[h, kind] = (
                        own[c][i, kind, rows, :]
                        + a[c][i, kind, rows, :].astype(jnp.float32)
                        + b[c][i, kind, rows, :].astype(jnp.float32)
                    ).astype(jnp.bfloat16)
            h += 1


def final_sum_call(core, own, a, b):
    vm = pl.BlockSpec(memory_space=pltpu.VMEM)
    shape = jax.ShapeDtypeStruct((4, 2, BLK, BLK), jnp.bfloat16)
    return pl.pallas_call(
        final_sum_kernel,
        in_specs=[pl.BlockSpec(memory_space=pltpu.SMEM)] + [vm] * (3 * len(CHUNKS)),
        out_specs=[vm, vm],
        out_shape=[shape, shape],
        cost_estimate=pl.CostEstimate(flops=0, bytes_accessed=3 << 20, transcendentals=0),
        compiler_params=pltpu.CompilerParams(vmem_limit_bytes=VMEM),
        name="final_sum",
    )(core, *own, *a, *b)


def home_kernel(scal, keep, got, full, *refs):
    n = len(CHUNKS)
    parts, (dk, dv, dq, tmp, sems) = refs[:n], refs[n:]
    core = scal[0]
    copies = []
    h = 4 * (1 - core)
    for c in range(n):
        dst = dq.at[:, pl.ds(h, CHUNKS[c])]
        copies.append(pltpu.make_async_copy(parts[c], dst, sems.at[c]))
        h += CHUNKS[c]
    for copy in copies:
        copy.start()
    for kind, out in enumerate((dk, dv)):
        for src, side in ((keep, core), (got, 1 - core)):
            for i in range(4):
                tmp[pl.ds(4 * side + i, BLK, stride=8), :] = src[i, kind].astype(jnp.float32)
        out[...] = tmp[...].reshape(BLK, 8, BLK).astype(jnp.bfloat16)
    for copy in copies:
        copy.wait()


def home_call(core, keep, got, full, parts):
    vm = pl.BlockSpec(memory_space=pltpu.VMEM)
    hbm = pl.BlockSpec(memory_space=pl.ANY)
    shape = jax.ShapeDtypeStruct((BLK, 8, BLK), jnp.bfloat16)
    return pl.pallas_call(
        home_kernel,
        in_specs=[pl.BlockSpec(memory_space=pltpu.SMEM), vm, vm, hbm] + [hbm] * len(parts),
        out_specs=[vm, vm, hbm],
        out_shape=[shape, shape, jax.ShapeDtypeStruct(full.shape, full.dtype)],
        scratch_shapes=[
            pltpu.VMEM((BLK * 8, BLK), jnp.float32),
            pltpu.SemaphoreType.DMA((len(parts),)),
        ],
        input_output_aliases={3: 2},
        compiler_params=pltpu.CompilerParams(vmem_limit_bytes=VMEM),
        cost_estimate=pl.CostEstimate(flops=0, bytes_accessed=3 << 20, transcendentals=0),
        name="home_heads",
    )(core, keep, got, full, *parts)


def chunk_kernel(
    scal, q_own, q_twin, g_own, g_twin, d_own, d_twin, start, kv_own, kv_a, kv_b,
    dq_own, dq_twin, dkv_own, dkv_a, dkv_b,
    kbuf, vbuf, dk, dv,
):
    core = scal[0]
    rows = BLK * 8
    for n, src in enumerate((kv_b, kv_a, kv_own)):
        kbuf[256 * n : 256 * (n + 1), :] = src[0]
        vbuf[256 * n : 256 * (n + 1), :] = src[1]
    dk[...] = jnp.zeros_like(dk)
    dv[...] = jnp.zeros_like(dv)
    nt = (((1,), (1,)), ((), ()))
    tn = (((0,), (0,)), ((), ()))
    tok = lax.broadcasted_iota(jnp.int32, (1, rows), 1) >> 3
    sides = ((q_own, g_own, d_own, dq_own), (q_twin, g_twin, d_twin, dq_twin))
    for slot, (q, g, d, dq) in enumerate(sides):
        rb = core if slot == 0 else 1 - core
        win = pl.ds(pl.multiple_of(rb * BLK, BLK), 5 * BLK)
        q_t = q[...].astype(jnp.float32).reshape(rows, BLK).astype(jnp.bfloat16)
        g_t = g[...].astype(jnp.float32).reshape(rows, BLK).astype(jnp.bfloat16)
        s = lax.dot_general(kbuf[win, :], q_t, nt, preferred_element_type=jnp.float32)
        u = lax.broadcasted_iota(jnp.int32, s.shape, 0)
        s = jnp.where(u >= start[rb], s, NEG)
        w = lax.broadcasted_iota(jnp.int32, (BLK, rows), 0)
        s = jnp.concatenate([s[: 4 * BLK], jnp.where(w <= tok, s[4 * BLK :], NEG)], axis=0)
        m = jnp.max(s, axis=0, keepdims=True)
        e = jnp.exp2((s - m) * (SCALE * math.log2(math.e)))
        p = e * (1.0 / jnp.sum(e, axis=0, keepdims=True))
        dp = lax.dot_general(vbuf[win, :], g_t, nt, preferred_element_type=jnp.float32)
        dsc = (p * (dp - d[...])).astype(jnp.bfloat16)
        dv[win, :] += jnp.dot(p.astype(jnp.bfloat16), g_t, preferred_element_type=jnp.float32)
        dk[win, :] += jnp.dot(dsc, q_t, preferred_element_type=jnp.float32)
        dqn = lax.dot_general(dsc, kbuf[win, :], tn, preferred_element_type=jnp.float32)
        dq[...] = (dqn * SCALE).reshape(BLK, 8, BLK).astype(jnp.bfloat16)
    for n, dst in enumerate((dkv_b, dkv_a, dkv_own)):
        dst[0] = (dk[256 * n : 256 * (n + 1), :] * SCALE).astype(dst.dtype)
        dst[1] = dv[256 * n : 256 * (n + 1), :].astype(dst.dtype)


def chained_kernel(*refs):
    chunk_kernel(*refs[:11], *refs[12:])


def delta_kernel(o, g, out):
    x = o[...].astype(jnp.float32) * g[...].astype(jnp.float32)
    ones = jnp.ones((8, 2 * BLK), jnp.bfloat16)
    for j in range(8):
        part = x[:, j].reshape(BLK, BLK)
        high = part.astype(jnp.bfloat16)
        low = (part - high.astype(jnp.float32)).astype(jnp.bfloat16)
        r = lax.dot_general(
            ones,
            jnp.concatenate([high, low], axis=1),
            (((1,), (1,)), ((), ())),
            preferred_element_type=jnp.float32,
        )
        out[j] = r[:1]


def delta_call(o4, g4):
    spec = pl.BlockSpec((16, 8, 8, BLK), lambda i: (i, 0, 0, 0))
    return pl.pallas_call(
        delta_kernel,
        grid=(BLK // 16,),
        in_specs=[spec, spec],
        out_specs=pl.BlockSpec((8, 1, BLK), lambda i: (0, 0, i)),
        out_shape=jax.ShapeDtypeStruct((8, 1, BLK * 8), jnp.float32),
        compiler_params=pltpu.CompilerParams(vmem_limit_bytes=DELTA_VMEM),
        cost_estimate=pl.CostEstimate(
            flops=1 << 21, bytes_accessed=4 << 20, transcendentals=0
        ),
        name="delta",
    )(o4, g4)


def chunk_call(
    core, h0, nh, q4, qt, g4, gt, d_own, d_twin, start, kv_own, kv_a, kv_b, dq
):
    rows = BLK * 8
    own = pl.BlockSpec((BLK, None, 8, BLK), lambda h, s: (0, 4 * s[0] + h0 + h, 0, 0))
    d_o = pl.BlockSpec((None, 1, rows), lambda h, s: (4 * s[0] + h0 + h, 0, 0))
    st = pl.BlockSpec((2, 1, rows), lambda h, s: (0, 0, 0))
    kvc = pl.BlockSpec((None, 2, 256, BLK), lambda h, s: (h, 0, 0, 0))
    dqs = pl.BlockSpec((BLK, None, 8, BLK), lambda h, s: (0, h, 0, 0))
    chain = [] if dq is None else [dq]
    return pl.pallas_call(
        chunk_kernel if dq is None else chained_kernel,
        grid_spec=pltpu.PrefetchScalarGridSpec(
            num_scalar_prefetch=1,
            grid=(nh,),
            in_specs=[own, own, own, own, d_o, d_o, st, kvc, kvc, kvc]
            + [pl.BlockSpec(memory_space=pl.ANY)] * len(chain),
            out_specs=[own, dqs, kvc, kvc, kvc],
            scratch_shapes=[
                pltpu.VMEM((768, BLK), jnp.bfloat16),
                pltpu.VMEM((768, BLK), jnp.bfloat16),
                pltpu.VMEM((768, BLK), jnp.float32),
                pltpu.VMEM((768, BLK), jnp.float32),
            ],
        ),
        out_shape=[
            jax.ShapeDtypeStruct((BLK, 8, 8, BLK), jnp.bfloat16),
            jax.ShapeDtypeStruct((BLK, nh, 8, BLK), jnp.bfloat16),
            jax.ShapeDtypeStruct((nh, 2, 256, BLK), jnp.float32),
            jax.ShapeDtypeStruct((nh, 2, 256, BLK), jnp.bfloat16),
            jax.ShapeDtypeStruct((nh, 2, 256, BLK), jnp.bfloat16),
        ],
        compiler_params=pltpu.CompilerParams(vmem_limit_bytes=VMEM),
        input_output_aliases={} if dq is None else {11: 0},
        cost_estimate=pl.CostEstimate(
            flops=nh * 2 * 5 * 2 * rows * 640 * 128,
            bytes_accessed=nh * (6 * rows * 256 + 7 * 131072),
            transcendentals=nh * 2 * rows * 640,
        ),
        name="attention_chunk",
    )(core, q4, qt, g4, gt, d_own, d_twin, start, kv_own, kv_a, kv_b, *chain)


def shards(queries, keys, values, outputs, out_grad, segments):
    dev = lax.axis_index("ctx") * lax.axis_size("head") + lax.axis_index("head")
    core = (dev & 1).reshape(1)
    chip = dev >> 1

    k_twin, v_twin = swap_cores(keys), swap_cores(values)
    seg_pad = jnp.concatenate([jnp.full((512,), -1, jnp.int32), segments])
    seg_w = lax.dynamic_slice_in_dim(seg_pad, chip * 256, 768, 0)
    rows = jnp.broadcast_to(seg_w[512:, None], (256, 8)).reshape(2, 1, BLK * 8)
    first = jnp.sum((seg_w[:, None, None, None] < rows[None]).astype(jnp.int32), axis=0)
    start = first - jnp.array([[[0]], [[BLK]]], jnp.int32)

    half = gather_call(core, 0, keys, values, [])
    k_twin, v_twin, start = lax.optimization_barrier((k_twin, v_twin, start))
    kv_own = gather_call(core, 1, k_twin, v_twin, half)
    queries, out_grad, outputs, *kv_own = lax.optimization_barrier(
        (queries, out_grad, outputs, *kv_own)
    )
    kv_a = [chip_shift(x, 1) for x in kv_own[:2]]
    kv_b = [chip_shift(x, 2) for x in kv_own[:2]]
    q4 = queries.reshape(BLK, 8, 8, BLK)
    g4 = out_grad.reshape(BLK, 8, 8, BLK)
    qt, gt = swap_cores(q4), swap_cores(g4)
    delta = delta_call(outputs.reshape(BLK, 8, 8, BLK), g4)
    d_twin = swap_cores(delta)

    dq, dq_twin, own, back_a, back_b = None, [], [], [], []
    h0 = 0
    for c, nh in enumerate(CHUNKS):
        if c >= 2:
            kv_own[c], own[c - 2] = lax.optimization_barrier((kv_own[c], own[c - 2]))
        if c >= len(kv_a):
            kv_a.append(chip_shift(kv_own[c], 1))
            kv_b.append(chip_shift(kv_own[c], 2))
        dq, t, dkv_o, dkv_a, dkv_b = chunk_call(
            core, h0, nh, q4, qt, g4, gt, delta, d_twin, start, kv_own[c], kv_a[c], kv_b[c], dq
        )
        h0 += nh
        own.append(dkv_o)
        if c:
            dkv_a, dkv_b, back_a[-1], back_b[-1] = lax.optimization_barrier(
                (dkv_a, dkv_b, back_a[-1], back_b[-1])
            )
        back_b.append(chip_shift(dkv_b, -2))
        back_a.append(chip_shift(dkv_a, -1))
        dq_twin.append(swap_cores(t))
    keep, send = final_sum_call(core, own, back_a, back_b)
    dkeys, dvals, dq = home_call(core, keep, swap_cores(send), dq, dq_twin)
    return dq.reshape(BLK, 64, BLK), dkeys, dvals


def solution(mesh):
    spec = P(AXES, None, None)
    return jax.shard_map(
        shards,
        mesh=mesh,
        in_specs=(spec, spec, spec, spec, spec, P()),
        out_specs=(spec, spec, spec),
        check_vma=False,
    )
```

```python
import functools
import math

import jax
import jax.numpy as jnp
from jax import lax
from jax.experimental import pallas as pl
from jax.experimental.pallas import tpu as pltpu
from jax.sharding import PartitionSpec as P

AXES = ("ctx", "head")
BLK = 128
NEG = -1e30
SCALE = BLK ** (-0.5)
CHUNKS = (2, 2)
VMEM = 28 << 20
DELTA_VMEM = 57 << 20


def chip_shift(x, chips):
    n = lax.axis_size("ctx") * lax.axis_size("head")
    return lax.ppermute(x, AXES, [(i, (i + 2 * chips) % n) for i in range(n)])


def swap_cores(x):
    n = lax.axis_size("ctx") * lax.axis_size("head")
    return lax.ppermute(x, AXES, [(i, i ^ 1) for i in range(n)])


def gather_kernel(slot, scal, k, v, *refs):
    outs, tmp = refs[-len(CHUNKS) - 1 : -1], refs[-1]
    core = scal[0]
    rb = core if slot == 0 else 1 - core
    rows = pl.ds(pl.multiple_of(rb * BLK, BLK), BLK)
    for kind, src in enumerate((k, v)):
        tmp[...] = src[...].astype(jnp.float32).reshape(BLK * 8, BLK)
        h = 0
        for out in outs:
            for i in range(out.shape[0]):
                part = tmp[pl.ds(4 * core + h, BLK, stride=8), :]
                out[i, kind, rows, :] = part.astype(jnp.bfloat16)
                h += 1


def gather_call(core, slot, k, v, chain):
    vm = pl.BlockSpec(memory_space=pltpu.VMEM)
    return pl.pallas_call(
        functools.partial(gather_kernel, slot),
        in_specs=[pl.BlockSpec(memory_space=pltpu.SMEM)] + [vm] * (2 + len(chain)),
        out_specs=[vm] * len(CHUNKS),
        out_shape=[jax.ShapeDtypeStruct((nh, 2, 256, BLK), jnp.bfloat16) for nh in CHUNKS],
        scratch_shapes=[pltpu.VMEM((BLK * 8, BLK), jnp.float32)],
        input_output_aliases={3 + i: i for i in range(len(chain))},
        compiler_params=pltpu.CompilerParams(vmem_limit_bytes=VMEM),
        cost_estimate=pl.CostEstimate(flops=0, bytes_accessed=1 << 19, transcendentals=0),
        name="gather_heads",
    )(core, k, v, *chain)


def final_sum_kernel(scal, *refs):
    n = len(CHUNKS)
    core = scal[0]
    own, a, b = refs[:n], refs[n : 2 * n], refs[2 * n : 3 * n]
    keep, send = refs[3 * n :]
    h = 0
    for c in range(n):
        for i in range(CHUNKS[c]):
            for kind in range(2):
                for out, rb in ((keep, core), (send, 1 - core)):
                    rows = pl.ds(pl.multiple_of(rb * BLK, BLK), BLK)
                    out[h, kind] = (
                        own[c][i, kind, rows, :]
                        + a[c][i, kind, rows, :].astype(jnp.float32)
                        + b[c][i, kind, rows, :].astype(jnp.float32)
                    ).astype(jnp.bfloat16)
            h += 1


def final_sum_call(core, own, a, b):
    vm = pl.BlockSpec(memory_space=pltpu.VMEM)
    shape = jax.ShapeDtypeStruct((4, 2, BLK, BLK), jnp.bfloat16)
    return pl.pallas_call(
        final_sum_kernel,
        in_specs=[pl.BlockSpec(memory_space=pltpu.SMEM)] + [vm] * (3 * len(CHUNKS)),
        out_specs=[vm, vm],
        out_shape=[shape, shape],
        cost_estimate=pl.CostEstimate(flops=0, bytes_accessed=3 << 20, transcendentals=0),
        compiler_params=pltpu.CompilerParams(vmem_limit_bytes=VMEM),
        name="final_sum",
    )(core, *own, *a, *b)


def home_kernel(scal, keep, got, full, *refs):
    n = len(CHUNKS)
    parts, (dk, dv, dq, tmp, sems) = refs[:n], refs[n:]
    core = scal[0]
    copies = []
    h = 4 * (1 - core)
    for c in range(n):
        dst = dq.at[:, pl.ds(h, CHUNKS[c])]
        copies.append(pltpu.make_async_copy(parts[c], dst, sems.at[c]))
        h += CHUNKS[c]
    for copy in copies:
        copy.start()
    for kind, out in enumerate((dk, dv)):
        for src, side in ((keep, core), (got, 1 - core)):
            for i in range(4):
                tmp[pl.ds(4 * side + i, BLK, stride=8), :] = src[i, kind].astype(jnp.float32)
        out[...] = tmp[...].reshape(BLK, 8, BLK).astype(jnp.bfloat16)
    for copy in copies:
        copy.wait()


def home_call(core, keep, got, full, parts):
    vm = pl.BlockSpec(memory_space=pltpu.VMEM)
    hbm = pl.BlockSpec(memory_space=pl.ANY)
    shape = jax.ShapeDtypeStruct((BLK, 8, BLK), jnp.bfloat16)
    return pl.pallas_call(
        home_kernel,
        in_specs=[pl.BlockSpec(memory_space=pltpu.SMEM), vm, vm, hbm] + [hbm] * len(parts),
        out_specs=[vm, vm, hbm],
        out_shape=[shape, shape, jax.ShapeDtypeStruct(full.shape, full.dtype)],
        scratch_shapes=[
            pltpu.VMEM((BLK * 8, BLK), jnp.float32),
            pltpu.SemaphoreType.DMA((len(parts),)),
        ],
        input_output_aliases={3: 2},
        compiler_params=pltpu.CompilerParams(vmem_limit_bytes=VMEM),
        cost_estimate=pl.CostEstimate(flops=0, bytes_accessed=3 << 20, transcendentals=0),
        name="home_heads",
    )(core, keep, got, full, *parts)


def chunk_kernel(
    scal, q_own, q_twin, g_own, g_twin, d_own, d_twin, start, kv_own, kv_a, kv_b,
    dq_own, dq_twin, dkv_own, dkv_a, dkv_b,
    kbuf, vbuf, dk, dv,
):
    core = scal[0]
    rows = BLK * 8
    for n, src in enumerate((kv_b, kv_a, kv_own)):
        kbuf[256 * n : 256 * (n + 1), :] = src[0]
        vbuf[256 * n : 256 * (n + 1), :] = src[1]
    dk[...] = jnp.zeros_like(dk)
    dv[...] = jnp.zeros_like(dv)
    nt = (((1,), (1,)), ((), ()))
    tn = (((0,), (0,)), ((), ()))
    tok = lax.broadcasted_iota(jnp.int32, (1, rows), 1) >> 3
    sides = ((q_own, g_own, d_own, dq_own), (q_twin, g_twin, d_twin, dq_twin))
    for slot, (q, g, d, dq) in enumerate(sides):
        rb = core if slot == 0 else 1 - core
        win = pl.ds(pl.multiple_of(rb * BLK, BLK), 5 * BLK)
        q_t = q[...].astype(jnp.float32).reshape(rows, BLK).astype(jnp.bfloat16)
        g_t = g[...].astype(jnp.float32).reshape(rows, BLK).astype(jnp.bfloat16)
        s = lax.dot_general(kbuf[win, :], q_t, nt, preferred_element_type=jnp.float32)
        u = lax.broadcasted_iota(jnp.int32, s.shape, 0)
        s = jnp.where(u >= start[rb], s, NEG)
        w = lax.broadcasted_iota(jnp.int32, (BLK, rows), 0)
        s = jnp.concatenate([s[: 4 * BLK], jnp.where(w <= tok, s[4 * BLK :], NEG)], axis=0)
        m = jnp.max(s, axis=0, keepdims=True)
        e = jnp.exp2((s - m) * (SCALE * math.log2(math.e)))
        p = e * (1.0 / jnp.sum(e, axis=0, keepdims=True))
        dp = lax.dot_general(vbuf[win, :], g_t, nt, preferred_element_type=jnp.float32)
        dsc = (p * (dp - d[...])).astype(jnp.bfloat16)
        dv[win, :] += jnp.dot(p.astype(jnp.bfloat16), g_t, preferred_element_type=jnp.float32)
        dk[win, :] += jnp.dot(dsc, q_t, preferred_element_type=jnp.float32)
        dqn = lax.dot_general(dsc, kbuf[win, :], tn, preferred_element_type=jnp.float32)
        dq[...] = (dqn * SCALE).reshape(BLK, 8, BLK).astype(jnp.bfloat16)
    for n, dst in enumerate((dkv_b, dkv_a, dkv_own)):
        dst[0] = (dk[256 * n : 256 * (n + 1), :] * SCALE).astype(dst.dtype)
        dst[1] = dv[256 * n : 256 * (n + 1), :].astype(dst.dtype)


def chained_kernel(*refs):
    chunk_kernel(*refs[:11], *refs[12:])


def delta_kernel(o, g, out):
    x = o[...].astype(jnp.float32) * g[...].astype(jnp.float32)
    ones = jnp.ones((8, 2 * BLK), jnp.bfloat16)
    for j in range(8):
        part = x[:, j].reshape(BLK, BLK)
        high = part.astype(jnp.bfloat16)
        low = (part - high.astype(jnp.float32)).astype(jnp.bfloat16)
        r = lax.dot_general(
            ones,
            jnp.concatenate([high, low], axis=1),
            (((1,), (1,)), ((), ())),
            preferred_element_type=jnp.float32,
        )
        out[j] = r[:1]


def delta_call(o4, g4):
    spec = pl.BlockSpec((16, 8, 8, BLK), lambda i: (i, 0, 0, 0))
    return pl.pallas_call(
        delta_kernel,
        grid=(BLK // 16,),
        in_specs=[spec, spec],
        out_specs=pl.BlockSpec((8, 1, BLK), lambda i: (0, 0, i)),
        out_shape=jax.ShapeDtypeStruct((8, 1, BLK * 8), jnp.float32),
        compiler_params=pltpu.CompilerParams(vmem_limit_bytes=DELTA_VMEM),
        cost_estimate=pl.CostEstimate(
            flops=1 << 21, bytes_accessed=4 << 20, transcendentals=0
        ),
        name="delta",
    )(o4, g4)


def chunk_call(
    core, h0, nh, q4, qt, g4, gt, d_own, d_twin, start, kv_own, kv_a, kv_b, dq
):
    rows = BLK * 8
    own = pl.BlockSpec((BLK, None, 8, BLK), lambda h, s: (0, 4 * s[0] + h0 + h, 0, 0))
    d_o = pl.BlockSpec((None, 1, rows), lambda h, s: (4 * s[0] + h0 + h, 0, 0))
    st = pl.BlockSpec((2, 1, rows), lambda h, s: (0, 0, 0))
    kvc = pl.BlockSpec((None, 2, 256, BLK), lambda h, s: (h, 0, 0, 0))
    dqs = pl.BlockSpec((BLK, None, 8, BLK), lambda h, s: (0, h, 0, 0))
    chain = [] if dq is None else [dq]
    return pl.pallas_call(
        chunk_kernel if dq is None else chained_kernel,
        grid_spec=pltpu.PrefetchScalarGridSpec(
            num_scalar_prefetch=1,
            grid=(nh,),
            in_specs=[own, own, own, own, d_o, d_o, st, kvc, kvc, kvc]
            + [pl.BlockSpec(memory_space=pl.ANY)] * len(chain),
            out_specs=[own, dqs, kvc, kvc, kvc],
            scratch_shapes=[
                pltpu.VMEM((768, BLK), jnp.bfloat16),
                pltpu.VMEM((768, BLK), jnp.bfloat16),
                pltpu.VMEM((768, BLK), jnp.float32),
                pltpu.VMEM((768, BLK), jnp.float32),
            ],
        ),
        out_shape=[
            jax.ShapeDtypeStruct((BLK, 8, 8, BLK), jnp.bfloat16),
            jax.ShapeDtypeStruct((BLK, nh, 8, BLK), jnp.bfloat16),
            jax.ShapeDtypeStruct((nh, 2, 256, BLK), jnp.float32),
            jax.ShapeDtypeStruct((nh, 2, 256, BLK), jnp.bfloat16),
            jax.ShapeDtypeStruct((nh, 2, 256, BLK), jnp.bfloat16),
        ],
        compiler_params=pltpu.CompilerParams(vmem_limit_bytes=VMEM),
        input_output_aliases={} if dq is None else {11: 0},
        cost_estimate=pl.CostEstimate(
            flops=nh * 2 * 5 * 2 * rows * 640 * 128,
            bytes_accessed=nh * (6 * rows * 256 + 7 * 131072),
            transcendentals=nh * 2 * rows * 640,
        ),
        name="attention_chunk",
    )(core, q4, qt, g4, gt, d_own, d_twin, start, kv_own, kv_a, kv_b, *chain)


def shards(queries, keys, values, outputs, out_grad, segments):
    dev = lax.axis_index("ctx") * lax.axis_size("head") + lax.axis_index("head")
    core = (dev & 1).reshape(1)
    chip = dev >> 1

    k_twin, v_twin = swap_cores(keys), swap_cores(values)
    seg_pad = jnp.concatenate([jnp.full((512,), -1, jnp.int32), segments])
    seg_w = lax.dynamic_slice_in_dim(seg_pad, chip * 256, 768, 0)
    rows = jnp.broadcast_to(seg_w[512:, None], (256, 8)).reshape(2, 1, BLK * 8)
    first = jnp.sum((seg_w[:, None, None, None] < rows[None]).astype(jnp.int32), axis=0)
    start = first - jnp.array([[[0]], [[BLK]]], jnp.int32)

    half = gather_call(core, 0, keys, values, [])
    k_twin, v_twin, start = lax.optimization_barrier((k_twin, v_twin, start))
    kv_own = gather_call(core, 1, k_twin, v_twin, half)
    queries, out_grad, outputs, *kv_own = lax.optimization_barrier(
        (queries, out_grad, outputs, *kv_own)
    )
    kv_a = [chip_shift(x, 1) for x in kv_own[:2]]
    kv_b = [chip_shift(x, 2) for x in kv_own[:2]]
    q4 = queries.reshape(BLK, 8, 8, BLK)
    g4 = out_grad.reshape(BLK, 8, 8, BLK)
    qt, gt = swap_cores(q4), swap_cores(g4)
    delta = delta_call(outputs.reshape(BLK, 8, 8, BLK), g4)
    d_twin = swap_cores(delta)

    dq, dq_twin, own, back_a, back_b = None, [], [], [], []
    h0 = 0
    for c, nh in enumerate(CHUNKS):
        if c >= 2:
            kv_own[c], own[c - 2] = lax.optimization_barrier((kv_own[c], own[c - 2]))
        if c >= len(kv_a):
            kv_a.append(chip_shift(kv_own[c], 1))
            kv_b.append(chip_shift(kv_own[c], 2))
        dq, t, dkv_o, dkv_a, dkv_b = chunk_call(
            core, h0, nh, q4, qt, g4, gt, delta, d_twin, start, kv_own[c], kv_a[c], kv_b[c], dq
        )
        h0 += nh
        own.append(dkv_o)
        if c:
            dkv_b, dkv_a, back_b[-1], back_a[-1] = lax.optimization_barrier(
                (dkv_b, dkv_a, back_b[-1], back_a[-1])
            )
        back_a.append(chip_shift(dkv_a, -1))
        back_b.append(chip_shift(dkv_b, -2))
        dq_twin.append(swap_cores(t))
    keep, send = final_sum_call(core, own, back_b, back_a)
    dkeys, dvals, dq = home_call(core, keep, swap_cores(send), dq, dq_twin)
    return dq.reshape(BLK, 64, BLK), dkeys, dvals


def solution(mesh):
    spec = P(AXES, None, None)
    return jax.shard_map(
        shards,
        mesh=mesh,
        in_specs=(spec, spec, spec, spec, spec, P()),
        out_specs=(spec, spec, spec),
        check_vma=False,
    )
```
